512 devices in a mesh: blk: 64 (over y_lo, z, core), rep: 8 (over y_hi, x).
Axes of the slice: x: 4, y: 8 (y_hi: 2, y_lo: 4; y = y_hi * 4 + y_lo), z: 8, core: 2. Of those that a mesh axis runs over, the one named last changes fastest.
Arguments:
- hidden_in: bfloat16 [8, 8192, 1536], P('rep', 'blk'), may hold values from -12 to 12
- lengths: int32 [512], P('rep'), may hold values from 1 to 128, 32768 in all
- routes: int32 [8, 8192, 8], P('rep', 'blk'), may hold values from 0 to 31, all different within a row; in each aligned block of 128 rows (0 to 127, 128 to 255, ..., all dimensions but the last counted through in order) at most 36 rows name the same one
- route_weights: float32 [8, 8192, 8], P('rep', 'blk'), may hold values from 0.03 to 0.3
- norm_gain: float32 [1536], replicated, may hold values from 0.1 to 1.9
- master: float32 [3, 1536, 64, 256], P(None, 'blk', None, 'rep'), may hold values from -1 to 1
- unembed: bfloat16 [32768, 1536], P('blk'), may hold values from -0.5 to 0.5
- final_gain: float32 [1536], replicated, may hold values from 0.5 to 1.5
- target_ids: int32 [512], P('rep'), may hold values from 0 to 32767
Outputs:
- hidden_out: bfloat16 [8, 8192, 1536], P('rep', 'blk')
- server_blocks: bfloat16 [3, 1536, 16384], P(None, None, 'blk')
- request_stats: float32 [3, 512], P(None, 'rep')
The draws below stay inside these ranges and needn't reach their ends.
Inputs may be any that keep to these rules, and one draw needn't show every extreme that they name: `routes`: in the 128 slots of one device no expert is named by more than 36 slots, and in some device one expert is named by exactly 36. The lengths of all 512 prompts sum to 32768 and the longest is exactly 128.
All inputs are finite; a program needn't handle non-finite values. No bound on the sum of `lengths` on one device may be relied on, other than what follows from the above.
Results may differ from the reference program's by a relative error of at most 0.0022.
Values may be sent and summed in bfloat16 or wider, within the bound.
A program may use at most 128 MiB of HBM per device.

```python
import math
import jax
import jax.numpy as jnp
import numpy as np
from jax import lax

D = 1536
FF = 512
EXPERTS = 32
TOP = 8
VOCAB = 32768
LEN = 128
ROWS = 128
CAP = 36
UNITS_DEV = 256
UNIT_BLOCKS = 64
TOKENS_REP = 8192
PROMPTS_REP = 64
REPLICAS = 8
PROMPTS = 512
TOKENS = 65536
N_BLK = 64


def draw_hidden_in(key, part):
    values = jnp.clip(jax.random.normal(key, (REPLICAS, TOKENS_REP, D), jnp.float32), -4.0, 4.0)
    position = (jnp.arange(TOKENS_REP) % LEN).astype(jnp.float32)
    rising = 1.0 + 2.0 * position / LEN
    return (values * rising[None, :, None]).astype(jnp.bfloat16)


def draw_master(key, part):
    shape_all = (3, D, UNIT_BLOCKS, UNITS_DEV)
    values = jnp.clip(jax.random.normal(key, shape_all, jnp.float32), -4.0, 4.0)
    fan_in = jnp.array([D, D, FF], jnp.float32)
    return (values * (fan_in ** (-0.5))[:, None, None, None]).astype(jnp.float32)


def with_ends(values, rng, smallest, largest):
    index_at = [jax.random.randint(jax.random.fold_in(rng, axis), (), 0, length) for axis, length in enumerate(values.shape)]
    main_axis = values.shape.index(max(values.shape))
    neighbour = index_at[:main_axis] + [(index_at[main_axis] + 1) % values.shape[main_axis]] + index_at[main_axis + 1:]
    return values.at[tuple(index_at)].set(smallest).at[tuple(neighbour)].set(largest)


def levels(own_key, shape, shards, low, top_value):
    factor_of, own = 1.0, jax.random.fold_in(own_key, 6)
    for dim, parts in shards:
        heights = jnp.exp(jax.random.uniform(jax.random.fold_in(own, dim), (parts,), jnp.float32, low / len(shards), top_value / len(shards)))
        factor_of = factor_of * jnp.repeat(heights, shape[dim] // parts).reshape([-1 if axis == dim else 1 for axis in range(len(shape))])
    return factor_of


def cumulative_ranks(number_of, lean):
    weights = [(1 << 20) // math.isqrt(grade ** lean) + 1 for grade in range(1, number_of + 1)]
    deviation = 1 + sum(weights) // (1 << 30)
    return np.cumsum(np.array([max(1, weight // deviation) for weight in weights]))


def skewed_ids(stream_key, dims, number_of, lean):
    grid = cumulative_ranks(number_of, lean)
    lot = jax.random.randint(jax.random.fold_in(stream_key, 1), dims, 0, int(grid[number_of - 1]))
    standing = jnp.searchsorted(jnp.asarray(grid, jnp.int32), lot, side="right")
    return jax.random.permutation(jax.random.fold_in(stream_key, 2), number_of)[standing].astype(jnp.int32)


def profile(amount, total, limit, lean):
    portions = [(1 << 20) // math.isqrt(standing ** lean) + 1 for standing in range(2, amount + 1)]
    spare, given = total - limit - (amount - 1), [1] * (amount - 1)
    while spare > 0:
        free = [i for i in range(amount - 1) if given[i] < limit]
        mass, budget = sum([portions[i] for i in free]), spare
        for i in free:
            addition = min(limit - given[i], max(1, budget * portions[i] // mass), spare)
            given[i] = given[i] + addition
            spare = spare - addition
    return np.array([limit] + given)


def ragged(stream_key, amount, total, bound, slope):
    if amount == 2:
        one = jax.random.randint(stream_key, (), max(1, total - bound), min(bound, total - 1) + 1)
        return jnp.stack([one, total - one])
    sizes = jnp.asarray(profile(amount, total, bound, slope), jnp.int32)
    pairs = (amount - 1) // 2
    giver, sink = sizes[1:1 + 2 * pairs:2], sizes[2:2 + 2 * pairs:2]
    slack = jnp.minimum(giver - 1, bound - sink)
    shifted = jax.random.randint(jax.random.fold_in(stream_key, 1), (pairs,), 0, 1 << 20) % (slack + 1)
    sizes = sizes.at[1:1 + 2 * pairs:2].set(giver - shifted).at[2:2 + 2 * pairs:2].set(sink + shifted)
    return sizes[jax.random.permutation(jax.random.fold_in(stream_key, 2), amount)]


def assign_block(key, own, number, rows, number_of, top, bound, skew):
    order = jax.random.permutation(key, number_of)
    packed, common = load_shares(number_of, rows * top, bound, skew, True), load_shares(number_of, rows * top, bound, skew, False)
    places = jnp.arange(number_of)

    def named(sizes, offset_by):
        used = int((sizes > 0).sum())
        fixed = max(1, used // 4)
        passed = fixed + (places - fixed + offset_by * (used - fixed)) % max(1, number_of - fixed)
        return jnp.zeros((number_of,), jnp.int32).at[order[jnp.where(places < fixed, places, passed)]].set(jnp.asarray(sizes, jnp.int32))

    sizes = jnp.where(number % 4 == 0, named(packed, number // 4), named(common, number - number // 4 - 1))
    mixed = jax.random.permutation(jax.random.fold_in(own, 3), number_of)
    giver, taker = mixed[0:number_of // 2 * 2:2], mixed[1:number_of // 2 * 2:2]
    slack = jnp.minimum(sizes[giver] - 1, bound - sizes[taker]) // 2
    slack = jnp.where((giver == order[0]) | (taker == order[0]) | (sizes[taker] == 0), 0, jnp.maximum(slack, 0))
    passed = jax.random.randint(jax.random.fold_in(own, 4), (number_of // 2,), 0, 1 << 20) % (slack + 1)
    sizes = sizes.at[giver].add(-passed).at[taker].add(passed)
    members = jnp.searchsorted(jnp.cumsum(sizes), jnp.arange(rows * top), side="right").astype(jnp.int32)
    grid = members.reshape(top, rows).T
    grid = grid[jax.random.permutation(jax.random.fold_in(own, 1), rows)]
    offset_by = jax.random.randint(jax.random.fold_in(own, 2), (rows, 1), 0, top)
    return jnp.take_along_axis(grid, (jnp.arange(top)[None, :] + offset_by) % top, axis=1)


def load_shares(number_of, total, limit, skew, full):
    loads = [(1 << 20) // math.isqrt(grade ** skew) + 1 for grade in range(1, number_of + 1)]
    largest = limit if full else min(limit, max(-(-total // number_of), total * loads[0] // sum(loads)))
    least = 1 if total - largest >= number_of - 1 else 0
    given, surplus = [largest] + [least] * (number_of - 1), total - largest - least * (number_of - 1)
    while surplus > 0:
        free = [i for i in range(1, number_of) if given[i] < largest] or [i for i in range(1, number_of) if given[i] < limit]
        pool, remaining = sum([loads[i] for i in free]), surplus
        for i in free:
            more = min(limit - given[i], max(1, remaining * loads[i] // pool), surplus)
            given[i] = given[i] + more
            surplus = surplus - more
    return np.array(given)


def centred(key, dims, spread, limit, shards=(), kind=jnp.bfloat16):
    factor_of = levels(key, dims, shards, -0.22, 0.18) if shards else 1.0
    drawn = jax.random.normal(key, dims, jnp.float32) * spread * factor_of
    return jnp.minimum(jnp.maximum(drawn, -limit), limit).astype(kind)


def setup_inputs(seed: int = 0) -> dict:
    arg_keys = jax.random.split(jax.random.key(seed), 10)
    hidden_in = draw_hidden_in(jax.random.fold_in(arg_keys[9], 71), 0)
    lengths = ragged(arg_keys[1], PROMPTS, PROMPTS * LEN // 2, LEN, 2).astype(jnp.int32)
    routes_keys = jax.random.split(jax.random.fold_in(arg_keys[2], 1), REPLICAS * TOKENS_REP // ROWS)
    routes_turns = jax.random.permutation(jax.random.fold_in(arg_keys[2], 3), REPLICAS * TOKENS_REP // ROWS)
    routes = jax.vmap(lambda own, number: assign_block(jax.random.fold_in(arg_keys[2], 2), own, number, ROWS, EXPERTS, TOP, CAP, 2))(routes_keys, routes_turns).reshape((REPLICAS, TOKENS_REP, TOP))
    route_weights = jnp.clip(jnp.exp(math.log(0.3) - 2.3025852 * jax.random.uniform(arg_keys[3], (REPLICAS, TOKENS_REP, TOP), jnp.float32) ** levels(arg_keys[3], (REPLICAS, TOKENS_REP, TOP), ((0, 8), (1, 64)), -0.2, 0.2)), 0.03, 0.3)
    norm_gain = jnp.clip(1.0 + 0.18 * jax.random.normal(arg_keys[4], (D,), jnp.float32), 0.1, 1.9)
    master = draw_master(jax.random.fold_in(arg_keys[9], 71), 0)
    unembed = centred(arg_keys[6], (VOCAB, D), 0.08, 0.5, ((0, 64),))
    final_gain = jnp.clip(1.0 + 0.1 * jax.random.normal(arg_keys[7], (D,), jnp.float32), 0.5, 1.5)
    target_ids = with_ends(skewed_ids(arg_keys[8], (PROMPTS,), VOCAB, 2), jax.random.fold_in(arg_keys[8], 3), 0, VOCAB - 1).astype(jnp.int32)
    return dict(hidden_in=hidden_in, lengths=lengths, routes=routes, route_weights=route_weights, norm_gain=norm_gain, master=master, unembed=unembed, final_gain=final_gain, target_ids=target_ids)


def reference(hidden_in, lengths, routes, route_weights, norm_gain, master, unembed, final_gain, target_ids):
    unit_count = EXPERTS * FF // N_BLK
    group_width = min(unit_count, FF)
    server = master.astype(jnp.bfloat16).reshape(3, D, EXPERTS * FF)
    tokens_all = hidden_in.reshape(TOKENS, D)
    token_index = jnp.arange(TOKENS, dtype=jnp.int32)
    slot_index = token_index % TOKENS_REP
    prompt_of = token_index // TOKENS_REP * PROMPTS_REP + slot_index // LEN
    position = slot_index % LEN
    row_len = lengths[prompt_of]
    is_valid = position < row_len
    resid_f = tokens_all.astype(jnp.float32)
    normed = (resid_f * lax.rsqrt(lax.optimization_barrier(jnp.mean(resid_f * resid_f, axis=-1, keepdims=True)) + 1e-05) * norm_gain).astype(jnp.bfloat16)
    choices_all = routes.reshape(TOKENS, TOP)
    weight_all = route_weights.reshape(TOKENS, TOP) * is_valid[:, None].astype(jnp.float32)
    most_rows = TOKENS // ROWS * CAP

    def per_expert(expert, total):
        expert = jnp.asarray(expert).astype(jnp.int32)
        match = choices_all == expert
        weight_row = lax.optimization_barrier(jnp.sum(jnp.where(match, weight_all, 0.0), axis=1))
        chosen = jnp.any(match, axis=1)
        picked = jnp.nonzero(chosen, size=most_rows, fill_value=0)[0].astype(jnp.int32)
        live = jnp.arange(most_rows) < jnp.sum(chosen)
        weight_pick = jnp.where(live, weight_row[picked], 0.0)
        rows_in = normed[picked]
        start_col = (expert * FF).astype(jnp.int32)
        gate_cols = lax.dynamic_slice_in_dim(server[0], start_col, FF, 1)
        up_cols = lax.dynamic_slice_in_dim(server[1], start_col, FF, 1)
        down_cols = lax.dynamic_slice_in_dim(server[2], start_col, FF, 1)
        gate_out = jnp.dot(rows_in, gate_cols, preferred_element_type=jnp.float32)
        up_out = jnp.dot(rows_in, up_cols, preferred_element_type=jnp.float32)
        hidden = (jax.nn.silu(gate_out) * up_out).astype(jnp.bfloat16)
        expert_out = jnp.zeros((most_rows, D), jnp.float32)
        for start in range(0, FF, group_width):
            piece_out = jnp.dot(hidden[:, start:start + group_width], down_cols[:, start:start + group_width].T, preferred_element_type=jnp.float32).astype(jnp.bfloat16)
            piece_out = lax.optimization_barrier(piece_out)
            expert_out = expert_out + piece_out.astype(jnp.float32)
        expert_round = lax.optimization_barrier(expert_out.astype(jnp.bfloat16))
        return total.at[picked].add(expert_round.astype(jnp.float32) * weight_pick[:, None])
    moe = lax.fori_loop(0, EXPERTS, per_expert, jnp.zeros((TOKENS, D), jnp.float32))
    out_rows = (resid_f + moe).astype(jnp.bfloat16)
    hidden_out = out_rows.reshape(REPLICAS, TOKENS_REP, D)
    out_f = out_rows.astype(jnp.float32)
    row_squares = lax.optimization_barrier(jnp.sum(out_f * out_f, axis=-1)) * is_valid.astype(jnp.float32)
    square_sums = jax.ops.segment_sum(row_squares, prompt_of, num_segments=PROMPTS)
    norms = jnp.sqrt(square_sums / (lengths.astype(jnp.float32) * D) + 1e-06)
    prompt_ids = jnp.arange(PROMPTS, dtype=jnp.int32)
    last_index = prompt_ids // PROMPTS_REP * TOKENS_REP + prompt_ids % PROMPTS_REP * LEN + lengths.astype(jnp.int32) - 1
    last_rows = out_f[last_index]
    final = (last_rows * lax.rsqrt(lax.optimization_barrier(jnp.mean(last_rows * last_rows, axis=-1, keepdims=True)) + 1e-05) * final_gain).astype(jnp.bfloat16)
    logits = jnp.dot(final, unembed.T, preferred_element_type=jnp.float32)
    top_logit = lax.optimization_barrier(jnp.max(logits, axis=1))
    target_logit = jnp.take_along_axis(logits, target_ids.astype(jnp.int32)[:, None], axis=1)[:, 0]
    request_stats = jnp.stack([norms, top_logit, target_logit])
    return (hidden_out, server, request_stats)
```

```python
import functools

import jax
import jax.numpy as jnp
from jax import lax
from jax.experimental import pallas as pl
from jax.experimental.pallas import tpu as pltpu
from jax.sharding import PartitionSpec as P

FF = 512
EXPERTS = 32
LEN = 128
CAP = 36
MESH = pl.DeviceIdType.MESH


def greet(count, me):
    barrier = pltpu.get_barrier_semaphore()

    def signal(i, carry):
        peer = lax.rem(me + i, count)
        pl.semaphore_signal(barrier, inc=1, device_id={"blk": peer}, device_id_type=MESH)
        return carry

    lax.fori_loop(1, count, signal, 0)
    pl.semaphore_wait(barrier, count - 1)


def exchange(count, me, make):
    def send(i, carry):
        make(lax.rem(me + i, count), me).start()
        return carry

    def finish(i, carry):
        make(lax.rem(me + i, count), lax.rem(me + i, count)).wait()
        return carry

    lax.fori_loop(1, count, send, 0)
    lax.fori_loop(1, count, finish, 0)


def tail_kernel(
    count, width, row_ref, unembed_ref, target_ref, length_ref, out_ref,
    rows, parts, send_a, recv_a, send_b, recv_b,
):
    me = lax.axis_index("blk")
    greet(count, me)
    rows[me] = row_ref[...]

    def row_copy(peer, slot):
        return pltpu.make_async_remote_copy(
            src_ref=row_ref, dst_ref=rows.at[slot], send_sem=send_a.at[peer],
            recv_sem=recv_a.at[slot], device_id={"blk": peer}, device_id_type=MESH,
        )

    exchange(count, me, row_copy)
    gathered = rows[...].reshape(count, width + 128)
    final = gathered[:, :width].astype(jnp.bfloat16)
    logits = lax.dot_general(
        unembed_ref[...], final, (((1,), (1,)), ((), ())), preferred_element_type=jnp.float32
    )
    vocab = lax.broadcasted_iota(jnp.int32, logits.shape, 0) + me * logits.shape[0]
    hit = vocab == target_ref[...]
    top = jnp.max(logits, axis=0, keepdims=True)
    target = jnp.sum(jnp.where(hit, logits, 0.0), axis=0, keepdims=True)
    parts[me] = jnp.concatenate([top, target], axis=0)

    def part_copy(peer, slot):
        return pltpu.make_async_remote_copy(
            src_ref=parts.at[me], dst_ref=parts.at[slot], send_sem=send_b.at[peer],
            recv_sem=recv_b.at[slot], device_id={"blk": peer}, device_id_type=MESH,
        )

    exchange(count, me, part_copy)
    squares = gathered[:, width : width + count]
    diagonal = lax.broadcasted_iota(jnp.int32, squares.shape, 0) == lax.broadcasted_iota(
        jnp.int32, squares.shape, 1
    )
    square = jnp.sum(jnp.where(diagonal, squares, 0.0), axis=0, keepdims=True)
    lengths = length_ref[...].astype(jnp.float32)
    out_ref[0:1, :] = jnp.sqrt(square / (lengths * width) + 1e-06)
    everything = parts[...]
    out_ref[1:2, :] = jnp.max(everything[:, 0, :], axis=0, keepdims=True)
    out_ref[2:3, :] = jnp.sum(everything[:, 1, :], axis=0, keepdims=True)


def tail(row, unembed, target_ids, lengths, count):
    width = unembed.shape[1]
    vmem = pl.BlockSpec(memory_space=pltpu.VMEM)
    return pl.pallas_call(
        functools.partial(tail_kernel, count, width),
        out_shape=jax.ShapeDtypeStruct((3, count), jnp.float32),
        in_specs=[vmem] * 4,
        out_specs=vmem,
        scratch_shapes=[
            pltpu.VMEM((count, 1, width + 128), jnp.float32),
            pltpu.VMEM((count, 2, count), jnp.float32),
            pltpu.SemaphoreType.DMA((count,)),
            pltpu.SemaphoreType.DMA((count,)),
            pltpu.SemaphoreType.DMA((count,)),
            pltpu.SemaphoreType.DMA((count,)),
        ],
        compiler_params=pltpu.CompilerParams(
            collective_id=1, has_side_effects=True, vmem_limit_bytes=32 << 20
        ),
    )(row, unembed, target_ids[None], lengths[None])


def local(
    hidden_in, lengths, routes, route_weights, norm_gain, master, unembed, final_gain, target_ids
):
    rows_here, width = hidden_in.shape[1:]
    blk_count = lax.axis_size("blk")
    blk_index = lax.axis_index("blk")
    blocks = master.astype(jnp.bfloat16)
    arrived_blocks = lax.all_to_all(blocks, "blk", split_axis=2, concat_axis=1, tiled=True)
    server = lax.all_gather(arrived_blocks, "rep", axis=3, tiled=True)[:, :, 0, :]
    partner = lax.ppermute(server, "blk", [(i, i ^ 1) for i in range(blk_count)])

    row_len = jnp.sum(
        jnp.where(jnp.arange(lengths.shape[0], dtype=jnp.int32) == blk_index, lengths, 0)
    )
    position = jnp.arange(rows_here, dtype=jnp.int32)
    is_valid = position < row_len
    resid_f = hidden_in[0].astype(jnp.float32)
    normed = (
        resid_f * lax.rsqrt(jnp.mean(resid_f * resid_f, axis=-1, keepdims=True) + 1e-05) * norm_gain
    ).astype(jnp.bfloat16)
    named = routes[0][:, :, None] == jnp.arange(EXPERTS, dtype=jnp.int32)
    named = named & is_valid[:, None, None]
    weight = jnp.sum(jnp.where(named, route_weights[0][:, :, None], 0.0), axis=1)
    hits = jnp.any(named, axis=1)
    before = (position[:, None] > position[None, :]).astype(jnp.bfloat16)
    rank = lax.dot_general(
        before, hits.astype(jnp.bfloat16), (((1,), (0,)), ((), ())),
        preferred_element_type=jnp.float32,
    ).astype(jnp.int32)
    place = hits[:, :, None] & (rank[:, :, None] == jnp.arange(CAP, dtype=jnp.int32))
    picker = place.reshape(rows_here, EXPERTS * CAP)
    sending = lax.dot_general(
        picker.astype(jnp.bfloat16), normed, (((0,), (0,)), ((), ())),
        preferred_element_type=jnp.float32,
    ).astype(jnp.bfloat16).reshape(EXPERTS, CAP, width)
    groups = [list(range(0, blk_count, 2)), list(range(1, blk_count, 2))]
    arrived = lax.all_to_all(
        sending, "blk", split_axis=0, concat_axis=0, tiled=True, axis_index_groups=groups
    )

    def half(rows, blocks):
        gate_out = jnp.dot(rows, blocks[0], preferred_element_type=jnp.float32)
        up_out = jnp.dot(rows, blocks[1], preferred_element_type=jnp.float32)
        hidden = (jax.nn.silu(gate_out) * up_out).astype(jnp.bfloat16)
        part = lax.dot_general(
            hidden, blocks[2], (((1,), (1,)), ((), ())), preferred_element_type=jnp.float32
        )
        return lax.reduce_precision(part, 8, 7)

    flat = arrived.reshape(EXPERTS * CAP, width)
    expert_out = (half(flat, server) + half(flat, partner)).astype(jnp.bfloat16)
    returned = lax.all_to_all(
        expert_out.reshape(EXPERTS, CAP, width), "blk", split_axis=0, concat_axis=0, tiled=True,
        axis_index_groups=groups,
    ).reshape(EXPERTS * CAP, width)
    spread = jnp.where(place, weight[:, :, None], 0.0).reshape(rows_here, EXPERTS * CAP)
    moe = 0.0
    left = spread
    for _ in range(3):
        piece = lax.reduce_precision(left, 8, 7)
        left = left - piece
        moe = moe + jnp.dot(
            piece.astype(jnp.bfloat16), returned, preferred_element_type=jnp.float32
        )
    out_rows = (resid_f + moe).astype(jnp.bfloat16)
    out_f = out_rows.astype(jnp.float32)
    square = jnp.sum(jnp.where(is_valid[:, None], out_f * out_f, 0.0))
    last = jnp.sum(jnp.where((position == row_len - 1)[:, None], out_f, 0.0), axis=0)
    final = last * lax.rsqrt(jnp.mean(last * last) + 1e-05) * final_gain
    final = lax.reduce_precision(final, 8, 7)
    row = jnp.concatenate([final, jnp.full((128,), square)])[None]
    request_stats = tail(row, unembed, target_ids, lengths, blk_count)
    return (out_rows[None], server, request_stats)


def solution(mesh):
    return jax.shard_map(
        local,
        mesh=mesh,
        in_specs=(
            P("rep", "blk", None),
            P("rep"),
            P("rep", "blk", None),
            P("rep", "blk", None),
            P(),
            P(None, "blk", None, "rep"),
            P("blk", None),
            P(),
            P("rep"),
        ),
        out_specs=(P("rep", "blk", None), P(None, None, "blk"), P(None, "rep")),
        check_vma=False,
    )
```
